32 devices in a mesh: groups: 2 (over y), ops: 16 (over z, x, core).
Axes of the slice: x: 2, y: 2, z: 4, core: 2. Of those that a mesh axis runs over, the one named last changes fastest.
Arguments:
- normal_ops: bfloat16 [256, 640, 640], P(('groups', 'ops')), parts along dimension 0, may hold values from -6 to 6
- rotation_one: bfloat16 [5120, 640], P(('groups', 'ops')), parts along dimension 0, may hold values from -0.25 to 0.25
- rotation_two: bfloat16 [5120, 640], P(('groups', 'ops')), parts along dimension 0, may hold values from -0.25 to 0.25
- integrals: float32 [64, 32], P('groups'), parts along dimension 0, may hold values from -1 to 1
- orbital_map: int32 [64], P('groups'), parts along dimension 0, may hold values from 0 to 31, each once
- couplings: int32 [8, 2], P('groups'), parts along dimension 0, may hold values from 0 to 3, as said below
- particles: int32 [8], P('groups'), parts along dimension 0, may hold values from 0 to 64
- state_counts: int32 [8], P('groups'), parts along dimension 0, may hold values from 320 to 640
Outputs:
- normal_next: bfloat16 [256, 640, 640], P(('groups', 'ops')), parts along dimension 0
- complementary_next: bfloat16 [256, 640, 640], P(('groups', 'ops')), parts along dimension 0
The draws below stay inside these ranges and needn't reach their ends.
There are 2 independent parts, one for each index of `groups`. The reference program is written for one: setup_inputs(seed, part) draws one part's arguments, and reference() takes and returns one part's arrays. A program takes and returns all parts, laid end to end along the dimension named above; each array names one. Nothing has to cross between parts.
Inputs may be any that keep to these rules, and one draw needn't show every extreme that they name: `couplings`: each row holds a source sector and a different target sector.
All inputs are finite; a program needn't handle non-finite values.
Results may differ from the reference program's by a relative error of at most 0.0075.
Values may be sent and summed in bfloat16 or wider, within the bound.
A program may use at most 128 MiB of HBM per device.

```python
import jax
import jax.numpy as jnp
from jax import lax

ORBS = 32
STATES = 640
SECTORS = 4
COUPLINGS = 4
BLOCKS = 128


def draw_couplings(key, part):
    first_key, second_key = jax.random.split(jax.random.fold_in(key, 11))
    source = jax.random.randint(first_key, (COUPLINGS,), 0, SECTORS)
    stride = jax.random.randint(second_key, (COUPLINGS,), 1, SECTORS)
    target = (source + stride) % SECTORS
    return jnp.stack([source, target], axis=1).astype(jnp.int32)


def set_ends(values, stream_key, least, largest):
    dims = values.shape
    place = [jax.random.randint(jax.random.fold_in(stream_key, axis), (), 0, dims[axis]) for axis in range(len(dims))]
    values = values.at[tuple(place)].set(least)
    longest = dims.index(max(dims))
    place[longest] = (place[longest] + 1) % dims[longest]
    return values.at[tuple(place)].set(largest)


def level_of(key, dims, cuts, smallest, top_value):
    loudness = 1.0
    for position, blocks in cuts:
        steps = jax.random.uniform(jax.random.fold_in(jax.random.fold_in(key, 6), position), (blocks,), jnp.float32, smallest / len(cuts), top_value / len(cuts))
        loudness = loudness * jnp.repeat(jnp.exp(steps), dims[position] // blocks).reshape((-1,) + (1,) * (len(dims) - 1 - position))
    return loudness


def centred(rng, extent, width, most, cuts=(), kind=jnp.bfloat16):
    entries = width * jax.random.normal(rng, extent, jnp.float32)
    if cuts:
        entries = entries * level_of(rng, extent, cuts, -0.22, 0.18)
    return jnp.clip(entries, -most, most).astype(kind)


def setup_inputs(seed: int = 0, part: int = 0) -> dict:
    arg_keys = jax.random.split(jax.random.key(seed), 9)
    part_keys = jax.random.split(jax.random.fold_in(arg_keys[8], part), 9)
    return {
        "normal_ops": centred(part_keys[0], (BLOCKS, STATES, STATES), 1.0, 6.0, ((0, 16),)),
        "rotation_one": centred(part_keys[1], (SECTORS * STATES, STATES), STATES ** -0.5, 0.25, ((0, 16),)),
        "rotation_two": centred(part_keys[2], (SECTORS * STATES, STATES), STATES ** -0.5, 0.25, ((0, 16),)),
        "integrals": centred(part_keys[3], (ORBS, ORBS), ORBS ** -0.5, 1.0, (), jnp.float32),
        "orbital_map": jax.random.permutation(part_keys[4], ORBS).astype(jnp.int32),
        "couplings": draw_couplings(jax.random.fold_in(jax.random.fold_in(arg_keys[8], part), 71), part),
        "particles": set_ends(jax.random.randint(part_keys[6], (SECTORS,), 0, 2 * ORBS + 1), jax.random.fold_in(part_keys[6], 1), 0, 2 * ORBS).astype(jnp.int32),
        "state_counts": set_ends(jax.random.randint(part_keys[7], (SECTORS,), STATES // 2, STATES + 1), jax.random.fold_in(part_keys[7], 1), STATES // 2, STATES).astype(jnp.int32),
    }


def rotate(blocks, basis, live_mask, source, target):
    frames = basis.reshape(SECTORS, STATES, STATES)

    def single(packed):
        block_data, from_sector, to_sector = packed
        frame_in = lax.dynamic_index_in_dim(frames, from_sector, 0, keepdims=False)
        frame_out = lax.dynamic_index_in_dim(frames, to_sector, 0, keepdims=False)
        keep_in = lax.dynamic_index_in_dim(live_mask, from_sector, 0, keepdims=False)
        keep_out = lax.dynamic_index_in_dim(live_mask, to_sector, 0, keepdims=False)
        half_turn = (jnp.dot(block_data, frame_in, preferred_element_type=jnp.float32) * keep_in[None, :]).astype(jnp.bfloat16)
        rotated = lax.dot_general(frame_out, half_turn, (((0,), (0,)), ((), ())), preferred_element_type=jnp.float32)
        return (rotated * keep_out[:, None]).astype(jnp.bfloat16)

    return lax.map(single, (blocks, source, target))


def reference(normal_ops, rotation_one, rotation_two, integrals, orbital_map, couplings, particles, state_counts):
    live_mask = (jnp.arange(STATES, dtype=jnp.int32)[None, :] < state_counts[:, None]).astype(jnp.float32)
    link_index = jnp.arange(ORBS * COUPLINGS, dtype=jnp.int32) % COUPLINGS
    source = couplings[link_index, 0].astype(jnp.int32)
    target = couplings[link_index, 1].astype(jnp.int32)
    normal_mid = rotate(normal_ops, rotation_one, live_mask, source, target)
    weights = integrals[:, orbital_map].astype(jnp.bfloat16)
    parity = (1 - 2 * (particles[couplings[:, 0]] % 2)).astype(jnp.float32)
    grouped = normal_mid.reshape(ORBS, COUPLINGS, STATES * STATES).astype(jnp.float32)
    mixture = jnp.einsum("ko,ocn->kcn", weights.astype(jnp.float32), grouped, precision=lax.Precision.HIGHEST)
    complementary_mid = (mixture * parity[None, :, None]).astype(jnp.bfloat16).reshape(ORBS * COUPLINGS, STATES, STATES)
    normal_next = rotate(normal_mid, rotation_two, live_mask, source, target)
    complementary_next = rotate(complementary_mid, rotation_two, live_mask, source, target)
    return normal_next, complementary_next
```

```python
import jax
import jax.numpy as jnp
from jax import lax
from jax.experimental import pallas as pl
from jax.experimental.pallas import tpu as pltpu
from jax.sharding import PartitionSpec as P


def select_entries(lookup, wanted):
    matches = wanted[:, None] == jnp.arange(lookup.shape[0], dtype=jnp.int32)[None, :]
    return jnp.sum(jnp.where(matches, lookup[None, :], 0), axis=1)


def rotate(blocks, basis, live_mask, source, target):
    sectors = live_mask.shape[0]
    states = live_mask.shape[1]
    frames = basis.reshape(sectors, states, states)

    def single(packed):
        block_data, from_sector, to_sector = packed
        frame_in = lax.dynamic_index_in_dim(frames, from_sector, 0, keepdims=False)
        frame_out = lax.dynamic_index_in_dim(frames, to_sector, 0, keepdims=False)
        keep_in = lax.dynamic_index_in_dim(live_mask, from_sector, 0, keepdims=False)
        keep_out = lax.dynamic_index_in_dim(live_mask, to_sector, 0, keepdims=False)
        half_turn = (
            jnp.dot(block_data, frame_in, preferred_element_type=jnp.float32) * keep_in[None, :]
        ).astype(jnp.bfloat16)
        rotated = lax.dot_general(
            frame_out, half_turn, (((0,), (0,)), ((), ())), preferred_element_type=jnp.float32
        )
        return (rotated * keep_out[:, None]).astype(jnp.bfloat16)

    return lax.map(single, (blocks, source, target))


def fetch_second(rotation_two):
    return lax.all_gather(rotation_two, "ops", axis=0, tiled=True)


def local_general(
    normal_ops,
    rotation_one,
    rotation_two,
    integrals,
    orbital_map,
    couplings,
    particles,
    state_counts,
):
    own_blocks = normal_ops.shape[0]
    states = normal_ops.shape[1]
    orbits = integrals.shape[0]
    link_count = couplings.shape[0]
    devices = lax.axis_size("ops")
    live_mask = (jnp.arange(states, dtype=jnp.int32)[None, :] < state_counts[:, None]).astype(
        jnp.float32
    )
    block_ids = lax.axis_index("ops") * own_blocks + jnp.arange(own_blocks, dtype=jnp.int32)
    link_of = block_ids % link_count
    source = select_entries(couplings[:, 0], link_of)
    target = select_entries(couplings[:, 1], link_of)
    basis_two = None
    basis_one = lax.all_gather(rotation_one, "ops", axis=0, tiled=True)
    normal_mid = rotate(normal_ops, basis_one, live_mask, source, target)
    normal_next = None
    chosen = (orbital_map[:, None] == jnp.arange(orbits, dtype=jnp.int32)[None, :]).astype(
        jnp.float32
    )
    weights = jnp.dot(integrals, chosen.T, precision=lax.Precision.HIGHEST).astype(jnp.bfloat16)
    parity = (1 - 2 * (select_entries(particles, couplings[:, 0]) % 2)).astype(jnp.float32)
    piece_len = states * states // devices
    spread = normal_mid.reshape(own_blocks, devices, piece_len)
    received = lax.all_to_all(spread, "ops", split_axis=1, concat_axis=0, tiled=True)
    entries = received.shape[2]
    grouped = received.reshape(orbits, link_count, entries)
    mixture = jnp.einsum("ko,ocn->kcn", weights, grouped, preferred_element_type=jnp.float32)
    regrouped = lax.all_to_all(
        (mixture * parity[None, :, None])
        .astype(jnp.bfloat16)
        .reshape(orbits * link_count, 1, entries),
        "ops",
        split_axis=0,
        concat_axis=1,
        tiled=True,
    )
    complementary_mid = regrouped.reshape(own_blocks, states, states)
    basis_two = fetch_second(rotation_two)
    normal_next = rotate(normal_mid, basis_two, live_mask, source, target)
    complementary_next = rotate(complementary_mid, basis_two, live_mask, source, target)
    return (normal_next, complementary_next)


SUB = 8


def mix_kernel(weights_ref, entries_ref, mixed_ref):
    orbits, rows, states = entries_ref.shape
    weights = weights_ref[...]
    for start in range(0, rows, SUB):
        piece = entries_ref[:, start : start + SUB, :].astype(jnp.float32)
        piece = piece.reshape(orbits * SUB, states).astype(jnp.bfloat16)
        mixed = jnp.dot(weights, piece, preferred_element_type=jnp.float32)
        mixed_ref[:, start : start + SUB, :] = mixed.reshape(orbits, SUB, states).astype(
            jnp.bfloat16
        )


def mix(weights, entries):
    orbits, rows, states = entries.shape
    return pl.pallas_call(
        mix_kernel,
        out_shape=jax.ShapeDtypeStruct(entries.shape, jnp.bfloat16),
        cost_estimate=pl.CostEstimate(
            flops=2 * orbits * orbits * SUB * rows * states,
            bytes_accessed=4 * orbits * rows * states,
            transcendentals=0,
        ),
    )(weights, entries)


def turn_kernel(source_ref, target_ref, data_ref, frame_in_ref, frame_out_ref, out_ref):
    states = frame_in_ref.shape[1]
    data = data_ref[...]
    if data.ndim == 4:
        data = data.astype(jnp.float32).reshape(states, states).astype(jnp.bfloat16)
    else:
        data = data.reshape(states, states)
    half_turn = jnp.dot(data, frame_in_ref[0], preferred_element_type=jnp.float32)
    out_ref[0] = jnp.dot(
        frame_out_ref[0], half_turn.astype(jnp.bfloat16), preferred_element_type=jnp.float32
    ).astype(jnp.bfloat16)


def turn(data, frames, frames_t, source, target):
    states = frames.shape[1]
    links = source.shape[0]
    if data.ndim == 4:
        count = data.shape[1]
        spec = pl.BlockSpec((data.shape[0], 1) + data.shape[2:], lambda b, s, t: (0, b, 0, 0))
    else:
        count = data.shape[0]
        spec = pl.BlockSpec((1, states, states), lambda b, s, t: (b, 0, 0))
    return pl.pallas_call(
        turn_kernel,
        grid_spec=pltpu.PrefetchScalarGridSpec(
            num_scalar_prefetch=2,
            grid=(count,),
            in_specs=[
                spec,
                pl.BlockSpec((1, states, states), lambda b, s, t: (s[b % links], 0, 0)),
                pl.BlockSpec((1, states, states), lambda b, s, t: (t[b % links], 0, 0)),
            ],
            out_specs=pl.BlockSpec((1, states, states), lambda b, s, t: (b, 0, 0)),
        ),
        out_shape=jax.ShapeDtypeStruct((count, states, states), jnp.bfloat16),
        cost_estimate=pl.CostEstimate(
            flops=4 * count * states**3,
            bytes_accessed=8 * count * states**2,
            transcendentals=0,
        ),
    )(source, target, data, frames, frames_t)


def local(
    normal_ops,
    rotation_one,
    rotation_two,
    integrals,
    orbital_map,
    couplings,
    particles,
    state_counts,
):
    own_blocks, states, _ = normal_ops.shape
    orbits = integrals.shape[0]
    links = couplings.shape[0]
    sectors = state_counts.shape[0]
    devices = lax.axis_size("ops")
    own = own_blocks // links
    if own * links != own_blocks or states % (devices * SUB):
        return local_general(
            normal_ops,
            rotation_one,
            rotation_two,
            integrals,
            orbital_map,
            couplings,
            particles,
            state_counts,
        )
    rows = states // devices
    source, target = couplings[:, 0], couplings[:, 1]
    chosen = (orbital_map[:, None] == jnp.arange(orbits, dtype=jnp.int32)[None, :]).astype(
        jnp.float32
    )
    weights = jnp.dot(integrals, chosen.T, precision=lax.Precision.HIGHEST)
    parity = (1 - 2 * (select_entries(particles, source) % 2)).astype(jnp.float32)
    eye = jnp.eye(SUB, dtype=jnp.float32)
    spread_weights = (weights[:, None, :, None] * eye[None, :, None, :]).reshape(
        orbits * SUB, orbits * SUB
    )
    split = normal_ops.reshape(own, links, devices, rows, states).transpose(1, 2, 0, 3, 4)
    received = [
        lax.all_to_all(split[c], "ops", split_axis=0, concat_axis=0, tiled=True)
        for c in range(links)
    ]
    live = (
        jnp.arange(states, dtype=jnp.int32)[None, :] < state_counts[:, None]
    ).astype(jnp.bfloat16)[:, None, :]
    basis_one = lax.all_gather(rotation_one, "ops", axis=0, tiled=True)
    basis_two = lax.all_gather(rotation_two, "ops", axis=0, tiled=True)
    basis_one = basis_one.reshape(sectors, states, states) * live
    basis_two = basis_two.reshape(sectors, states, states) * live
    frames = jnp.einsum(
        "sij,sjk->sik", basis_one, basis_two, preferred_element_type=jnp.float32
    ).astype(jnp.bfloat16)
    frames_t = frames.swapaxes(1, 2)
    normal_next = turn(normal_ops, frames, frames_t, source, target)
    pieces = []
    for c in range(links):
        mixed = mix(
            (spread_weights * parity[c]).astype(jnp.bfloat16),
            received[c].reshape(orbits, rows, states),
        )
        back = lax.all_to_all(
            mixed.reshape(devices, own, rows, states), "ops", split_axis=0, concat_axis=0, tiled=True
        )
        pieces.append(turn(back, frames, frames_t, source[c : c + 1], target[c : c + 1]))
    complementary_next = jnp.stack(pieces, axis=1).reshape(own_blocks, states, states)
    return (normal_next, complementary_next)


def solution(mesh):
    placed = (
        P(("groups", "ops"), None, None),
        P(("groups", "ops"), None),
        P(("groups", "ops"), None),
        P("groups", None),
        P("groups"),
        P("groups", None),
        P("groups"),
        P("groups"),
    )
    return jax.shard_map(
        local,
        mesh=mesh,
        in_specs=placed,
        out_specs=(P(("groups", "ops"), None, None), P(("groups", "ops"), None, None)),
        check_vma=False,
    )
```

```python
import functools

import jax
import jax.numpy as jnp
from jax import lax
from jax.experimental import pallas as pl
from jax.experimental.pallas import tpu as pltpu
from jax.sharding import PartitionSpec as P


def select_entries(lookup, wanted):
    matches = wanted[:, None] == jnp.arange(lookup.shape[0], dtype=jnp.int32)[None, :]
    return jnp.sum(jnp.where(matches, lookup[None, :], 0), axis=1)


def rotate(blocks, basis, live_mask, source, target):
    sectors = live_mask.shape[0]
    states = live_mask.shape[1]
    frames = basis.reshape(sectors, states, states)

    def single(packed):
        block_data, from_sector, to_sector = packed
        frame_in = lax.dynamic_index_in_dim(frames, from_sector, 0, keepdims=False)
        frame_out = lax.dynamic_index_in_dim(frames, to_sector, 0, keepdims=False)
        keep_in = lax.dynamic_index_in_dim(live_mask, from_sector, 0, keepdims=False)
        keep_out = lax.dynamic_index_in_dim(live_mask, to_sector, 0, keepdims=False)
        half_turn = (
            jnp.dot(block_data, frame_in, preferred_element_type=jnp.float32) * keep_in[None, :]
        ).astype(jnp.bfloat16)
        rotated = lax.dot_general(
            frame_out, half_turn, (((0,), (0,)), ((), ())), preferred_element_type=jnp.float32
        )
        return (rotated * keep_out[:, None]).astype(jnp.bfloat16)

    return lax.map(single, (blocks, source, target))


def fetch_second(rotation_two):
    return lax.all_gather(rotation_two, "ops", axis=0, tiled=True)


def local_general(
    normal_ops,
    rotation_one,
    rotation_two,
    integrals,
    orbital_map,
    couplings,
    particles,
    state_counts,
):
    own_blocks = normal_ops.shape[0]
    states = normal_ops.shape[1]
    orbits = integrals.shape[0]
    link_count = couplings.shape[0]
    devices = lax.axis_size("ops")
    live_mask = (jnp.arange(states, dtype=jnp.int32)[None, :] < state_counts[:, None]).astype(
        jnp.float32
    )
    block_ids = lax.axis_index("ops") * own_blocks + jnp.arange(own_blocks, dtype=jnp.int32)
    link_of = block_ids % link_count
    source = select_entries(couplings[:, 0], link_of)
    target = select_entries(couplings[:, 1], link_of)
    basis_two = None
    basis_one = lax.all_gather(rotation_one, "ops", axis=0, tiled=True)
    normal_mid = rotate(normal_ops, basis_one, live_mask, source, target)
    normal_next = None
    chosen = (orbital_map[:, None] == jnp.arange(orbits, dtype=jnp.int32)[None, :]).astype(
        jnp.float32
    )
    weights = jnp.dot(integrals, chosen.T, precision=lax.Precision.HIGHEST).astype(jnp.bfloat16)
    parity = (1 - 2 * (select_entries(particles, couplings[:, 0]) % 2)).astype(jnp.float32)
    piece_len = states * states // devices
    spread = normal_mid.reshape(own_blocks, devices, piece_len)
    received = lax.all_to_all(spread, "ops", split_axis=1, concat_axis=0, tiled=True)
    entries = received.shape[2]
    grouped = received.reshape(orbits, link_count, entries)
    mixture = jnp.einsum("ko,ocn->kcn", weights, grouped, preferred_element_type=jnp.float32)
    regrouped = lax.all_to_all(
        (mixture * parity[None, :, None])
        .astype(jnp.bfloat16)
        .reshape(orbits * link_count, 1, entries),
        "ops",
        split_axis=0,
        concat_axis=1,
        tiled=True,
    )
    complementary_mid = regrouped.reshape(own_blocks, states, states)
    basis_two = fetch_second(rotation_two)
    normal_next = rotate(normal_mid, basis_two, live_mask, source, target)
    complementary_next = rotate(complementary_mid, basis_two, live_mask, source, target)
    return (normal_next, complementary_next)


SUB = 8
LIMIT = 60 * 2**20
SHADOW = 400 * 2**20


def greet(devices):
    me = lax.axis_index("ops")
    barrier = pltpu.get_barrier_semaphore()

    @pl.loop(1, devices)
    def _(step):
        peer = lax.rem(me + step, devices)
        pl.semaphore_signal(
            barrier, inc=1, device_id={"ops": peer}, device_id_type=pl.DeviceIdType.MESH
        )

    pl.semaphore_wait(barrier, devices - 1)
    return me


def spread_kernel(
    devices, ops_ref, weights_ref, out_ref, landed, mixed, send_sem, recv_sem, keep_sem, out_sem
):
    links, _, own, rows, states = landed.shape
    me = greet(devices)

    def outgoing(link, peer):
        return pltpu.make_async_remote_copy(
            src_ref=ops_ref.at[:, link, peer],
            dst_ref=landed.at[link, me],
            send_sem=send_sem.at[link, peer],
            recv_sem=recv_sem.at[link, me],
            device_id={"ops": peer},
            device_id_type=pl.DeviceIdType.MESH,
        )

    def incoming(link, peer):
        return pltpu.make_async_remote_copy(
            src_ref=ops_ref.at[:, link, peer],
            dst_ref=landed.at[link, peer],
            send_sem=send_sem.at[link, peer],
            recv_sem=recv_sem.at[link, peer],
            device_id={"ops": peer},
            device_id_type=pl.DeviceIdType.MESH,
        )

    def kept(link):
        return pltpu.make_async_copy(
            ops_ref.at[:, link, me], landed.at[link, me], keep_sem.at[link]
        )

    @pl.loop(0, links)
    def _(link):
        kept(link).start()

        @pl.loop(1, devices)
        def _(step):
            outgoing(link, lax.rem(me + step, devices)).start()

    @pl.loop(0, links)
    def _(link):
        kept(link).wait()

        @pl.loop(1, devices)
        def _(step):
            incoming(link, lax.rem(me + step, devices)).wait_recv()

        weights = weights_ref[link]
        for start in range(0, rows, SUB):
            piece = landed[link, :, :, start : start + SUB, :].astype(jnp.float32)
            piece = piece.reshape(devices * own * SUB, states).astype(jnp.bfloat16)
            total = jnp.dot(weights, piece, preferred_element_type=jnp.float32)
            mixed[link, :, :, start : start + SUB, :] = total.reshape(
                devices, own, SUB, states
            ).astype(jnp.bfloat16)
        pltpu.make_async_copy(mixed.at[link], out_ref.at[link], out_sem.at[link]).start()

    @pl.loop(0, links)
    def _(link):
        pltpu.make_async_copy(mixed.at[link], out_ref.at[link], out_sem.at[link]).wait()

        @pl.loop(1, devices)
        def _(step):
            outgoing(link, lax.rem(me + step, devices)).wait_send()


def return_kernel(
    devices,
    couplings_ref,
    mixed_ref,
    ops_ref,
    one_ref,
    two_ref,
    live_ref,
    normal_ref,
    complementary_ref,
    landed,
    data,
    one,
    two,
    frames,
    frames_t,
    done,
    send_sem,
    recv_sem,
    keep_sem,
    load_sem,
    basis_sem,
    out_sem,
):
    links, own, _, rows, states = landed.shape
    sectors = frames.shape[0]
    blocks = data.shape[0]
    me = greet(devices)

    def copy_of(link, peer, slot):
        return pltpu.make_async_remote_copy(
            src_ref=mixed_ref.at[link, peer],
            dst_ref=landed.at[link, :, slot],
            send_sem=send_sem.at[link, peer],
            recv_sem=recv_sem.at[link, slot],
            device_id={"ops": peer},
            device_id_type=pl.DeviceIdType.MESH,
        )

    def kept(link):
        return pltpu.make_async_copy(
            mixed_ref.at[link, me], landed.at[link, :, me], keep_sem.at[link]
        )

    @pl.loop(0, links)
    def _(link):
        kept(link).start()

        @pl.loop(1, devices)
        def _(step):
            copy_of(link, lax.rem(me + step, devices), me).start()

    loads = (
        pltpu.make_async_copy(one_ref, one, basis_sem.at[0]),
        pltpu.make_async_copy(two_ref, two, basis_sem.at[1]),
        pltpu.make_async_copy(ops_ref, data, load_sem),
    )
    for load in loads:
        load.start()
    for load in loads:
        load.wait()

    @pl.loop(0, sectors)
    def _(sector):
        live = live_ref[sector]
        frame = (
            jnp.dot(one[sector] * live, two[sector] * live, preferred_element_type=jnp.float32)
        )
        frames[sector] = frame.astype(jnp.bfloat16)
        frames_t[sector] = frame.T.astype(jnp.bfloat16)

    def turn(block, link):
        half_turn = jnp.dot(
            block, frames[couplings_ref[link, 0]], preferred_element_type=jnp.float32
        )
        return jnp.dot(
            frames_t[couplings_ref[link, 1]],
            half_turn.astype(jnp.bfloat16),
            preferred_element_type=jnp.float32,
        ).astype(jnp.bfloat16)

    @pl.loop(0, blocks)
    def _(block):
        done[0, block] = turn(data[block], lax.rem(block, links))
        pltpu.make_async_copy(done.at[0, block], normal_ref.at[block], out_sem.at[0, block]).start()

    @pl.loop(0, links)
    def _(link):
        kept(link).wait()

        @pl.loop(1, devices)
        def _(step):
            peer = lax.rem(me + step, devices)
            copy_of(link, peer, peer).wait_recv()

        @pl.loop(0, own)
        def _(place):
            block = place * links + link
            piece = landed[link, place].astype(jnp.float32).reshape(states, states)
            done[1, block] = turn(piece.astype(jnp.bfloat16), link)
            pltpu.make_async_copy(
                done.at[1, block], complementary_ref.at[block], out_sem.at[1, block]
            ).start()

    @pl.loop(0, blocks)
    def _(block):
        pltpu.make_async_copy(done.at[0, block], normal_ref.at[block], out_sem.at[0, block]).wait()
        pltpu.make_async_copy(
            done.at[1, block], complementary_ref.at[block], out_sem.at[1, block]
        ).wait()

    @pl.loop(0, links)
    def _(link):
        @pl.loop(1, devices)
        def _(step):
            copy_of(link, lax.rem(me + step, devices), me).wait_send()


def local(
    normal_ops,
    rotation_one,
    rotation_two,
    integrals,
    orbital_map,
    couplings,
    particles,
    state_counts,
):
    own_blocks, states, _ = normal_ops.shape
    orbits = integrals.shape[0]
    links = couplings.shape[0]
    sectors = state_counts.shape[0]
    devices = lax.axis_size("ops")
    own = own_blocks // links
    if own * links != own_blocks or states % (devices * SUB):
        return local_general(
            normal_ops,
            rotation_one,
            rotation_two,
            integrals,
            orbital_map,
            couplings,
            particles,
            state_counts,
        )
    rows = states // devices
    source, target = couplings[:, 0], couplings[:, 1]
    chosen = (orbital_map[:, None] == jnp.arange(orbits, dtype=jnp.int32)[None, :]).astype(
        jnp.float32
    )
    weights = jnp.dot(integrals, chosen.T, precision=lax.Precision.HIGHEST)
    parity = (1 - 2 * (select_entries(particles, source) % 2)).astype(jnp.float32)
    eye = jnp.eye(SUB, dtype=jnp.float32)
    spread_weights = (weights[:, None, :, None] * eye[None, :, None, :]).reshape(
        orbits * SUB, orbits * SUB
    )
    ops_pieces = normal_ops.reshape(own, links, devices, rows, states)
    link_weights = (spread_weights[None] * parity[:, None, None]).astype(jnp.bfloat16)
    live = (
        jnp.arange(states, dtype=jnp.int32)[None, :] < state_counts[:, None]
    ).astype(jnp.bfloat16)[:, None, :]
    anywhere = pl.BlockSpec(memory_space=pl.ANY)
    vmem = pl.BlockSpec(memory_space=pltpu.VMEM)
    smem = pl.BlockSpec(memory_space=pltpu.SMEM)
    dma = pltpu.SemaphoreType.DMA
    basis_one = lax.all_gather(rotation_one, "ops", axis=0, tiled=True)
    basis_two = lax.all_gather(rotation_two, "ops", axis=0, tiled=True)
    mixed = pl.pallas_call(
        functools.partial(spread_kernel, devices),
        out_shape=jax.ShapeDtypeStruct((links, devices, own, rows, states), jnp.bfloat16),
        in_specs=[anywhere, vmem],
        out_specs=anywhere,
        scratch_shapes=[
            pltpu.VMEM((links, devices, own, rows, states), jnp.bfloat16),
            pltpu.VMEM((links, devices, own, rows, states), jnp.bfloat16),
            dma((links, devices)),
            dma((links, devices)),
            dma((links,)),
            dma((links,)),
        ],
        compiler_params=pltpu.CompilerParams(
            collective_id=0, has_side_effects=True, vmem_limit_bytes=LIMIT
        ),
        cost_estimate=pl.CostEstimate(flops=0, bytes_accessed=SHADOW, transcendentals=0),
    )(ops_pieces, link_weights)
    whole = (own_blocks, states, states)
    return pl.pallas_call(
        functools.partial(return_kernel, devices),
        out_shape=(
            jax.ShapeDtypeStruct(whole, jnp.bfloat16),
            jax.ShapeDtypeStruct(whole, jnp.bfloat16),
        ),
        in_specs=[smem, anywhere, anywhere, anywhere, anywhere, vmem],
        out_specs=(anywhere, anywhere),
        scratch_shapes=[
            pltpu.VMEM((links, own, devices, rows, states), jnp.bfloat16),
            pltpu.VMEM(whole, jnp.bfloat16),
            pltpu.VMEM((sectors, states, states), jnp.bfloat16),
            pltpu.VMEM((sectors, states, states), jnp.bfloat16),
            pltpu.VMEM((sectors, states, states), jnp.bfloat16),
            pltpu.VMEM((sectors, states, states), jnp.bfloat16),
            pltpu.VMEM((2,) + whole, jnp.bfloat16),
            dma((links, devices)),
            dma((links, devices)),
            dma((links,)),
            dma,
            dma((2,)),
            dma((2, own_blocks)),
        ],
        compiler_params=pltpu.CompilerParams(
            collective_id=1, has_side_effects=True, vmem_limit_bytes=LIMIT
        ),
        cost_estimate=pl.CostEstimate(flops=0, bytes_accessed=SHADOW, transcendentals=0),
    )(
        couplings,
        mixed,
        normal_ops,
        basis_one.reshape(sectors, states, states),
        basis_two.reshape(sectors, states, states),
        live,
    )


def solution(mesh):
    placed = (
        P(("groups", "ops"), None, None),
        P(("groups", "ops"), None),
        P(("groups", "ops"), None),
        P("groups", None),
        P("groups"),
        P("groups", None),
        P("groups"),
        P("groups"),
    )
    return jax.shard_map(
        local,
        mesh=mesh,
        in_specs=placed,
        out_specs=(P(("groups", "ops"), None, None), P(("groups", "ops"), None, None)),
        check_vma=False,
    )
```

```python
import functools

import jax
import jax.numpy as jnp
import numpy as np
from jax import lax
from jax.experimental import pallas as pl
from jax.experimental.pallas import tpu as pltpu
from jax.sharding import PartitionSpec as P


def select_entries(lookup, wanted):
    matches = wanted[:, None] == jnp.arange(lookup.shape[0], dtype=jnp.int32)[None, :]
    return jnp.sum(jnp.where(matches, lookup[None, :], 0), axis=1)


def rotate(blocks, basis, live_mask, source, target):
    sectors = live_mask.shape[0]
    states = live_mask.shape[1]
    frames = basis.reshape(sectors, states, states)

    def single(packed):
        block_data, from_sector, to_sector = packed
        frame_in = lax.dynamic_index_in_dim(frames, from_sector, 0, keepdims=False)
        frame_out = lax.dynamic_index_in_dim(frames, to_sector, 0, keepdims=False)
        keep_in = lax.dynamic_index_in_dim(live_mask, from_sector, 0, keepdims=False)
        keep_out = lax.dynamic_index_in_dim(live_mask, to_sector, 0, keepdims=False)
        half_turn = (
            jnp.dot(block_data, frame_in, preferred_element_type=jnp.float32) * keep_in[None, :]
        ).astype(jnp.bfloat16)
        rotated = lax.dot_general(
            frame_out, half_turn, (((0,), (0,)), ((), ())), preferred_element_type=jnp.float32
        )
        return (rotated * keep_out[:, None]).astype(jnp.bfloat16)

    return lax.map(single, (blocks, source, target))


def fetch_second(rotation_two):
    return lax.all_gather(rotation_two, "ops", axis=0, tiled=True)


def local_general(
    normal_ops,
    rotation_one,
    rotation_two,
    integrals,
    orbital_map,
    couplings,
    particles,
    state_counts,
):
    own_blocks = normal_ops.shape[0]
    states = normal_ops.shape[1]
    orbits = integrals.shape[0]
    link_count = couplings.shape[0]
    devices = lax.axis_size("ops")
    live_mask = (jnp.arange(states, dtype=jnp.int32)[None, :] < state_counts[:, None]).astype(
        jnp.float32
    )
    block_ids = lax.axis_index("ops") * own_blocks + jnp.arange(own_blocks, dtype=jnp.int32)
    link_of = block_ids % link_count
    source = select_entries(couplings[:, 0], link_of)
    target = select_entries(couplings[:, 1], link_of)
    basis_two = None
    basis_one = lax.all_gather(rotation_one, "ops", axis=0, tiled=True)
    normal_mid = rotate(normal_ops, basis_one, live_mask, source, target)
    normal_next = None
    chosen = (orbital_map[:, None] == jnp.arange(orbits, dtype=jnp.int32)[None, :]).astype(
        jnp.float32
    )
    weights = jnp.dot(integrals, chosen.T, precision=lax.Precision.HIGHEST).astype(jnp.bfloat16)
    parity = (1 - 2 * (select_entries(particles, couplings[:, 0]) % 2)).astype(jnp.float32)
    piece_len = states * states // devices
    spread = normal_mid.reshape(own_blocks, devices, piece_len)
    received = lax.all_to_all(spread, "ops", split_axis=1, concat_axis=0, tiled=True)
    entries = received.shape[2]
    grouped = received.reshape(orbits, link_count, entries)
    mixture = jnp.einsum("ko,ocn->kcn", weights, grouped, preferred_element_type=jnp.float32)
    regrouped = lax.all_to_all(
        (mixture * parity[None, :, None])
        .astype(jnp.bfloat16)
        .reshape(orbits * link_count, 1, entries),
        "ops",
        split_axis=0,
        concat_axis=1,
        tiled=True,
    )
    complementary_mid = regrouped.reshape(own_blocks, states, states)
    basis_two = fetch_second(rotation_two)
    normal_next = rotate(normal_mid, basis_two, live_mask, source, target)
    complementary_next = rotate(complementary_mid, basis_two, live_mask, source, target)
    return (normal_next, complementary_next)


SUB = 8
LIMIT = 62 * 2**20


def greet(devices):
    me = lax.axis_index("ops")
    barrier = pltpu.get_barrier_semaphore()

    @pl.loop(1, devices)
    def _(step):
        peer = lax.rem(me + step, devices)
        pl.semaphore_signal(
            barrier, inc=1, device_id={"ops": peer}, device_id_type=pl.DeviceIdType.MESH
        )

    pl.semaphore_wait(barrier, devices - 1)
    return me


def send(source, place, send_sem, recv_sem, peer):
    return pltpu.make_async_remote_copy(
        src_ref=source,
        dst_ref=place,
        send_sem=send_sem,
        recv_sem=recv_sem,
        device_id={"ops": peer},
        device_id_type=pl.DeviceIdType.MESH,
    )


def sweep_kernel(
    devices,
    couplings_ref,
    parity_ref,
    integrals_ref,
    chosen_ref,
    widen_ref,
    same_ref,
    live_ref,
    pieces_ref,
    ops_ref,
    one_ref,
    two_ref,
    normal_ref,
    complementary_ref,
    entries,
    stage,
    landed,
    data,
    one,
    two,
    own_frame,
    strips,
    frames,
    frames_t,
    done,
    send_one,
    recv_one,
    send_two,
    recv_two,
    send_basis,
    recv_basis,
    send_strip,
    recv_strip,
    send_relay,
    recv_relay,
    keep_one,
    keep_two,
    load_sem,
    stage_sem,
    out_sem,
):
    links, own, _, rows, states = landed.shape
    sectors = frames.shape[0]
    blocks = data.shape[0]
    team = devices // sectors
    me = greet(devices)
    sector, rank = lax.div(me, team), lax.rem(me, team)

    def basis_copy(peer_rank, slot):
        return send(
            two_ref,
            two.at[slot],
            send_basis.at[peer_rank],
            recv_basis.at[slot],
            sector * team + peer_rank,
        )

    def strip_copy(peer_sector, slot):
        return send(
            strips.at[slot * team + rank],
            strips.at[slot * team + rank],
            send_strip.at[peer_sector],
            recv_strip.at[slot],
            peer_sector * team + rank,
        )

    def relay_copy(peer_rank, of_sector, of_rank):
        return send(
            strips.at[of_sector * team + of_rank],
            strips.at[of_sector * team + of_rank],
            send_relay.at[peer_rank, of_sector],
            recv_relay.at[of_rank, of_sector],
            sector * team + peer_rank,
        )

    def entry_copy(link, peer, slot):
        return send(
            pieces_ref.at[:, link, peer],
            entries.at[link, slot],
            send_one.at[link, peer],
            recv_one.at[link, slot],
            peer,
        )

    def return_copy(link, peer, slot):
        return send(
            entries.at[link, peer],
            landed.at[link, :, slot],
            send_two.at[link, peer],
            recv_two.at[link, slot],
            peer,
        )

    def kept_one(link):
        return pltpu.make_async_copy(
            pieces_ref.at[:, link, me], entries.at[link, me], keep_one.at[link]
        )

    def kept_two(link):
        return pltpu.make_async_copy(
            entries.at[link, me], landed.at[link, :, me], keep_two.at[link]
        )

    @pl.loop(1, team)
    def _(step):
        basis_copy(lax.rem(rank + step, team), rank).start()

    @pl.loop(0, links)
    def _(link):
        kept_one(link).start()

        @pl.loop(1, devices)
        def _(step):
            entry_copy(link, lax.rem(me + step, devices), me).start()

    load_one = pltpu.make_async_copy(one_ref, one, load_sem.at[0])
    load_two = pltpu.make_async_copy(two_ref, two.at[rank], load_sem.at[1])
    load_data = pltpu.make_async_copy(ops_ref, data, load_sem.at[2])
    load_one.start()
    load_two.start()
    load_data.start()

    weights = jnp.dot(widen_ref[...], integrals_ref[...], preferred_element_type=jnp.float32)
    weights = jnp.dot(
        weights.astype(jnp.bfloat16), chosen_ref[...], preferred_element_type=jnp.float32
    )
    weights = weights * same_ref[...]

    load_one.wait()
    load_two.wait()

    @pl.loop(1, team)
    def _(step):
        peer_rank = lax.rem(rank + step, team)
        basis_copy(peer_rank, peer_rank).wait_recv()

    live = live_ref[sector]
    own_frame[...] = jnp.dot(
        one[...] * live,
        two[...].reshape(states, states) * live,
        preferred_element_type=jnp.float32,
    ).astype(jnp.bfloat16)
    own_strip = pltpu.make_async_copy(own_frame, strips.at[me], load_sem.at[3])
    own_strip.start()
    own_strip.wait()

    @pl.loop(1, sectors)
    def _(step):
        strip_copy(lax.rem(sector + step, sectors), sector).start()

    @pl.loop(0, links)
    def _(link):
        kept_one(link).wait()

        @pl.loop(1, devices)
        def _(step):
            peer = lax.rem(me + step, devices)
            entry_copy(link, peer, peer).wait_recv()

        signed = (weights * parity_ref[link]).astype(jnp.bfloat16)
        for start in range(0, rows, SUB):
            piece = entries[link, :, :, start : start + SUB, :].astype(jnp.float32)
            piece = piece.reshape(devices * own * SUB, states).astype(jnp.bfloat16)
            total = jnp.dot(signed, piece, preferred_element_type=jnp.float32)
            stage[:, :, start : start + SUB, :] = total.reshape(devices, own, SUB, states).astype(
                jnp.bfloat16
            )
        moved = pltpu.make_async_copy(stage, entries.at[link], stage_sem)
        moved.start()
        moved.wait()
        kept_two(link).start()

        @pl.loop(1, devices)
        def _(step):
            return_copy(link, lax.rem(me + step, devices), me).start()

    @pl.loop(1, sectors)
    def _(step):
        peer_sector = lax.rem(sector + step, sectors)
        strip_copy(peer_sector, peer_sector).wait_recv()

    @pl.loop(1, team)
    def _(step):
        peer_rank = lax.rem(rank + step, team)

        @pl.loop(0, sectors)
        def _(of_sector):
            relay_copy(peer_rank, of_sector, rank).start()

    load_data.wait()

    @pl.loop(1, team)
    def _(step):
        peer_rank = lax.rem(rank + step, team)

        @pl.loop(0, sectors)
        def _(of_sector):
            relay_copy(peer_rank, of_sector, peer_rank).wait_recv()

    @pl.loop(0, sectors)
    def _(index):
        frame = strips[pl.ds(index * team, team)].reshape(states, states)
        frames[index] = frame
        frames_t[index] = frame.astype(jnp.float32).T.astype(jnp.bfloat16)

    def turn(block, link):
        half_turn = jnp.dot(
            block, frames[couplings_ref[link, 0]], preferred_element_type=jnp.float32
        )
        return jnp.dot(
            frames_t[couplings_ref[link, 1]],
            half_turn.astype(jnp.bfloat16),
            preferred_element_type=jnp.float32,
        ).astype(jnp.bfloat16)

    def write(which, target, block):
        return pltpu.make_async_copy(
            done.at[which, block], target.at[block], out_sem.at[which, block]
        )

    @pl.loop(0, blocks)
    def _(block):
        done[0, block] = turn(data[block], lax.rem(block, links))
        write(0, normal_ref, block).start()

    @pl.loop(0, links)
    def _(link):
        kept_two(link).wait()

        @pl.loop(1, devices)
        def _(step):
            peer = lax.rem(me + step, devices)
            return_copy(link, peer, peer).wait_recv()

        @pl.loop(0, own)
        def _(place):
            block = place * links + link
            piece = landed[link, place].astype(jnp.float32).reshape(states, states)
            done[1, block] = turn(piece.astype(jnp.bfloat16), link)
            write(1, complementary_ref, block).start()

    @pl.loop(1, team)
    def _(step):
        peer_rank = lax.rem(rank + step, team)
        basis_copy(peer_rank, rank).wait_send()

        @pl.loop(0, sectors)
        def _(of_sector):
            relay_copy(peer_rank, of_sector, rank).wait_send()

    @pl.loop(1, sectors)
    def _(step):
        strip_copy(lax.rem(sector + step, sectors), sector).wait_send()

    @pl.loop(0, links)
    def _(link):
        @pl.loop(1, devices)
        def _(step):
            peer = lax.rem(me + step, devices)
            entry_copy(link, peer, me).wait_send()
            return_copy(link, peer, me).wait_send()

    @pl.loop(0, blocks)
    def _(block):
        write(0, normal_ref, block).wait()
        write(1, complementary_ref, block).wait()


def local(
    normal_ops,
    rotation_one,
    rotation_two,
    integrals,
    orbital_map,
    couplings,
    particles,
    state_counts,
):
    own_blocks, states, _ = normal_ops.shape
    orbits = integrals.shape[0]
    links = couplings.shape[0]
    sectors = state_counts.shape[0]
    devices = lax.axis_size("ops")
    own = own_blocks // links
    if own * links != own_blocks or states % (devices * SUB) or devices % sectors:
        return local_general(
            normal_ops,
            rotation_one,
            rotation_two,
            integrals,
            orbital_map,
            couplings,
            particles,
            state_counts,
        )
    rows = states // devices
    team = devices // sectors
    parity = (1 - 2 * (select_entries(particles, couplings[:, 0]) % 2)).astype(jnp.float32)
    wide = np.arange(orbits * SUB)
    widen = jnp.asarray(wide[:, None] // SUB == np.arange(orbits)[None, :], jnp.bfloat16)
    same = jnp.asarray(wide[:, None] % SUB == wide[None, :] % SUB, jnp.float32)
    chosen = (
        jnp.arange(orbits, dtype=jnp.int32)[:, None] == jnp.repeat(orbital_map, SUB)[None, :]
    ).astype(jnp.bfloat16)
    live = (
        jnp.arange(states, dtype=jnp.int32)[None, :] < state_counts[:, None]
    ).astype(jnp.bfloat16)[:, None, :]
    anywhere = pl.BlockSpec(memory_space=pl.ANY)
    vmem = pl.BlockSpec(memory_space=pltpu.VMEM)
    smem = pl.BlockSpec(memory_space=pltpu.SMEM)
    dma = pltpu.SemaphoreType.DMA
    whole = (own_blocks, states, states)
    strip = rotation_one.shape
    return pl.pallas_call(
        functools.partial(sweep_kernel, devices),
        out_shape=(
            jax.ShapeDtypeStruct(whole, jnp.bfloat16),
            jax.ShapeDtypeStruct(whole, jnp.bfloat16),
        ),
        in_specs=[smem, smem, vmem, vmem, vmem, vmem, vmem] + [anywhere] * 4,
        out_specs=(anywhere, anywhere),
        scratch_shapes=[
            pltpu.VMEM((links, devices, own, rows, states), jnp.bfloat16),
            pltpu.VMEM((devices, own, rows, states), jnp.bfloat16),
            pltpu.VMEM((links, own, devices, rows, states), jnp.bfloat16),
            pltpu.VMEM(whole, jnp.bfloat16),
            pltpu.VMEM(strip, jnp.bfloat16),
            pltpu.VMEM((team,) + strip, jnp.bfloat16),
            pltpu.VMEM(strip, jnp.bfloat16),
            pltpu.VMEM((devices,) + strip, jnp.bfloat16),
            pltpu.VMEM((sectors, states, states), jnp.bfloat16),
            pltpu.VMEM((sectors, states, states), jnp.bfloat16),
            pltpu.VMEM((2,) + whole, jnp.bfloat16),
            dma((links, devices)),
            dma((links, devices)),
            dma((links, devices)),
            dma((links, devices)),
            dma((team,)),
            dma((team,)),
            dma((sectors,)),
            dma((sectors,)),
            dma((team, sectors)),
            dma((team, sectors)),
            dma((links,)),
            dma((links,)),
            dma((4,)),
            dma,
            dma((2, own_blocks)),
        ],
        compiler_params=pltpu.CompilerParams(
            collective_id=0, has_side_effects=True, vmem_limit_bytes=LIMIT
        ),
    )(
        couplings,
        parity,
        integrals.astype(jnp.bfloat16),
        chosen,
        widen,
        same,
        live,
        normal_ops.reshape(own, links, devices, rows, states),
        normal_ops,
        rotation_one,
        rotation_two,
    )


def solution(mesh):
    placed = (
        P(("groups", "ops"), None, None),
        P(("groups", "ops"), None),
        P(("groups", "ops"), None),
        P("groups", None),
        P("groups"),
        P("groups", None),
        P("groups"),
        P("groups"),
    )
    return jax.shard_map(
        local,
        mesh=mesh,
        in_specs=placed,
        out_specs=(P(("groups", "ops"), None, None), P(("groups", "ops"), None, None)),
        check_vma=False,
    )
```

```python
import functools

import jax
import jax.numpy as jnp
import numpy as np
from jax import lax
from jax.experimental import pallas as pl
from jax.experimental.pallas import tpu as pltpu
from jax.sharding import PartitionSpec as P


def select_entries(lookup, wanted):
    matches = wanted[:, None] == jnp.arange(lookup.shape[0], dtype=jnp.int32)[None, :]
    return jnp.sum(jnp.where(matches, lookup[None, :], 0), axis=1)


def rotate(blocks, basis, live_mask, source, target):
    sectors = live_mask.shape[0]
    states = live_mask.shape[1]
    frames = basis.reshape(sectors, states, states)

    def single(packed):
        block_data, from_sector, to_sector = packed
        frame_in = lax.dynamic_index_in_dim(frames, from_sector, 0, keepdims=False)
        frame_out = lax.dynamic_index_in_dim(frames, to_sector, 0, keepdims=False)
        keep_in = lax.dynamic_index_in_dim(live_mask, from_sector, 0, keepdims=False)
        keep_out = lax.dynamic_index_in_dim(live_mask, to_sector, 0, keepdims=False)
        half_turn = (
            jnp.dot(block_data, frame_in, preferred_element_type=jnp.float32) * keep_in[None, :]
        ).astype(jnp.bfloat16)
        rotated = lax.dot_general(
            frame_out, half_turn, (((0,), (0,)), ((), ())), preferred_element_type=jnp.float32
        )
        return (rotated * keep_out[:, None]).astype(jnp.bfloat16)

    return lax.map(single, (blocks, source, target))


def fetch_second(rotation_two):
    return lax.all_gather(rotation_two, "ops", axis=0, tiled=True)


def local_general(
    normal_ops,
    rotation_one,
    rotation_two,
    integrals,
    orbital_map,
    couplings,
    particles,
    state_counts,
):
    own_blocks = normal_ops.shape[0]
    states = normal_ops.shape[1]
    orbits = integrals.shape[0]
    link_count = couplings.shape[0]
    devices = lax.axis_size("ops")
    live_mask = (jnp.arange(states, dtype=jnp.int32)[None, :] < state_counts[:, None]).astype(
        jnp.float32
    )
    block_ids = lax.axis_index("ops") * own_blocks + jnp.arange(own_blocks, dtype=jnp.int32)
    link_of = block_ids % link_count
    source = select_entries(couplings[:, 0], link_of)
    target = select_entries(couplings[:, 1], link_of)
    basis_two = None
    basis_one = lax.all_gather(rotation_one, "ops", axis=0, tiled=True)
    normal_mid = rotate(normal_ops, basis_one, live_mask, source, target)
    normal_next = None
    chosen = (orbital_map[:, None] == jnp.arange(orbits, dtype=jnp.int32)[None, :]).astype(
        jnp.float32
    )
    weights = jnp.dot(integrals, chosen.T, precision=lax.Precision.HIGHEST).astype(jnp.bfloat16)
    parity = (1 - 2 * (select_entries(particles, couplings[:, 0]) % 2)).astype(jnp.float32)
    piece_len = states * states // devices
    spread = normal_mid.reshape(own_blocks, devices, piece_len)
    received = lax.all_to_all(spread, "ops", split_axis=1, concat_axis=0, tiled=True)
    entries = received.shape[2]
    grouped = received.reshape(orbits, link_count, entries)
    mixture = jnp.einsum("ko,ocn->kcn", weights, grouped, preferred_element_type=jnp.float32)
    regrouped = lax.all_to_all(
        (mixture * parity[None, :, None])
        .astype(jnp.bfloat16)
        .reshape(orbits * link_count, 1, entries),
        "ops",
        split_axis=0,
        concat_axis=1,
        tiled=True,
    )
    complementary_mid = regrouped.reshape(own_blocks, states, states)
    basis_two = fetch_second(rotation_two)
    normal_next = rotate(normal_mid, basis_two, live_mask, source, target)
    complementary_next = rotate(complementary_mid, basis_two, live_mask, source, target)
    return (normal_next, complementary_next)


SUB = 8
LIMIT = 62 * 2**20


def greet(devices):
    me = lax.axis_index("ops")
    barrier = pltpu.get_barrier_semaphore()

    @pl.loop(1, devices)
    def _(step):
        peer = lax.rem(me + step, devices)
        pl.semaphore_signal(
            barrier, inc=1, device_id={"ops": peer}, device_id_type=pl.DeviceIdType.MESH
        )

    pl.semaphore_wait(barrier, devices - 1)
    return me


def send(source, place, send_sem, recv_sem, peer):
    return pltpu.make_async_remote_copy(
        src_ref=source,
        dst_ref=place,
        send_sem=send_sem,
        recv_sem=recv_sem,
        device_id={"ops": peer},
        device_id_type=pl.DeviceIdType.MESH,
    )


def sweep_kernel(
    devices,
    couplings_ref,
    particles_ref,
    counts_ref,
    orbital_ref,
    integrals_ref,
    widen_ref,
    same_ref,
    pieces_ref,
    ops_ref,
    one_ref,
    two_ref,
    normal_ref,
    complementary_ref,
    entries,
    stage,
    landed,
    data,
    one,
    two,
    own_frame,
    strips,
    frames,
    frames_t,
    done,
    chosen,
    send_one,
    recv_one,
    send_two,
    recv_two,
    send_basis,
    recv_basis,
    send_strip,
    recv_strip,
    send_relay,
    recv_relay,
    keep_one,
    keep_two,
    load_sem,
    stage_sem,
    out_sem,
):
    links, own, _, rows, states = landed.shape
    sectors = frames.shape[0]
    blocks = data.shape[0]
    team = devices // sectors
    me = greet(devices)
    sector, rank = lax.div(me, team), lax.rem(me, team)

    def basis_copy(peer_rank, slot):
        return send(
            two_ref,
            two.at[slot],
            send_basis.at[peer_rank],
            recv_basis.at[slot],
            sector * team + peer_rank,
        )

    half = sectors // 2
    across = lax.rem(sector + half, sectors)

    def strip_copy(peer_sector, slot):
        return send(
            strips.at[slot * team + rank],
            strips.at[slot * team + rank],
            send_strip.at[peer_sector, slot],
            recv_strip.at[slot],
            peer_sector * team + rank,
        )

    def neighbour(step):
        return lax.div(sector, half) * half + lax.rem(sector + step, half)

    def crossed(peer_sector):
        return lax.rem(peer_sector + half, sectors)

    def relay_copy(peer_rank, of_sector, of_rank):
        return send(
            strips.at[of_sector * team + of_rank],
            strips.at[of_sector * team + of_rank],
            send_relay.at[peer_rank, of_sector],
            recv_relay.at[of_rank, of_sector],
            sector * team + peer_rank,
        )

    def entry_copy(link, peer, slot):
        return send(
            pieces_ref.at[:, link, peer],
            entries.at[link, slot],
            send_one.at[link, peer],
            recv_one.at[link, slot],
            peer,
        )

    def return_copy(link, peer, slot):
        return send(
            entries.at[link, peer],
            landed.at[link, :, slot],
            send_two.at[link, peer],
            recv_two.at[link, slot],
            peer,
        )

    def kept_one(link):
        return pltpu.make_async_copy(
            pieces_ref.at[:, link, me], entries.at[link, me], keep_one.at[link]
        )

    def kept_two(link):
        return pltpu.make_async_copy(
            entries.at[link, me], landed.at[link, :, me], keep_two.at[link]
        )

    @pl.loop(1, team)
    def _(step):
        basis_copy(lax.rem(rank + step, team), rank).start()

    def send_entries(link):
        kept_one(link).start()

        @pl.loop(1, devices)
        def _(step):
            entry_copy(link, lax.rem(me + step, devices), me).start()

    send_entries(0)

    load_one = pltpu.make_async_copy(one_ref, one, load_sem.at[0])
    load_two = pltpu.make_async_copy(two_ref, two.at[rank], load_sem.at[1])
    load_data = pltpu.make_async_copy(ops_ref, data, load_sem.at[2])
    load_one.start()
    load_two.start()
    load_data.start()

    load_one.wait()
    load_two.wait()

    @pl.loop(1, team)
    def _(step):
        peer_rank = lax.rem(rank + step, team)
        basis_copy(peer_rank, peer_rank).wait_recv()

    columns = lax.broadcasted_iota(jnp.int32, (1, states), 1)
    live = (columns < counts_ref[sector]).astype(jnp.float32).astype(jnp.bfloat16)
    own_frame[...] = jnp.dot(
        one[...] * live,
        two[...].reshape(states, states) * live,
        preferred_element_type=jnp.float32,
    ).astype(jnp.bfloat16)
    own_strip = pltpu.make_async_copy(own_frame, strips.at[me], load_sem.at[3])
    own_strip.start()
    own_strip.wait()

    strip_copy(across, sector).start()

    @pl.loop(1, links)
    def _(link):
        send_entries(link)

    orbits = integrals_ref.shape[0]
    places = lax.broadcasted_iota(jnp.int32, (1, orbits), 1)
    for orbital in range(orbits):
        chosen[orbital : orbital + 1, :] = (places == orbital_ref[orbital]).astype(jnp.float32)
    weights = lax.dot_general(
        integrals_ref[...].astype(jnp.bfloat16),
        chosen[...].astype(jnp.bfloat16),
        (((1,), (1,)), ((), ())),
        preferred_element_type=jnp.float32,
    )
    weights = jnp.dot(
        widen_ref[...], weights.astype(jnp.bfloat16), preferred_element_type=jnp.float32
    )
    weights = lax.dot_general(
        weights.astype(jnp.bfloat16),
        widen_ref[...],
        (((1,), (1,)), ((), ())),
        preferred_element_type=jnp.float32,
    )
    weights = weights * same_ref[...]

    def mix_link(link):
        kept_one(link).wait()

        @pl.loop(1, devices)
        def _(step):
            peer = lax.rem(me + step, devices)
            entry_copy(link, peer, peer).wait_recv()

        parity = (1 - 2 * lax.rem(particles_ref[couplings_ref[0, link]], 2)).astype(jnp.float32)
        signed = (weights * parity).astype(jnp.bfloat16)
        for start in range(0, rows, SUB):
            piece = entries[link, :, :, start : start + SUB, :].astype(jnp.float32)
            piece = piece.reshape(devices * own * SUB, states).astype(jnp.bfloat16)
            total = jnp.dot(signed, piece, preferred_element_type=jnp.float32)
            stage[:, :, start : start + SUB, :] = total.reshape(devices, own, SUB, states).astype(
                jnp.bfloat16
            )
        moved = pltpu.make_async_copy(stage, entries.at[link], stage_sem)
        moved.start()
        moved.wait()
        kept_two(link).start()

        @pl.loop(1, devices)
        def _(step):
            return_copy(link, lax.rem(me + step, devices), me).start()

    mix_link(0)
    strip_copy(across, across).wait_recv()

    @pl.loop(1, half)
    def _(step):
        strip_copy(neighbour(step), sector).start()
        strip_copy(neighbour(step), across).start()

    @pl.loop(1, min(2, links))
    def _(link):
        mix_link(link)

    @pl.loop(1, half)
    def _(step):
        strip_copy(neighbour(step), neighbour(step)).wait_recv()
        strip_copy(neighbour(step), crossed(neighbour(step))).wait_recv()

    @pl.loop(1, team)
    def _(step):
        peer_rank = lax.rem(rank + step, team)

        @pl.loop(0, sectors)
        def _(of_sector):
            relay_copy(peer_rank, of_sector, rank).start()

    @pl.loop(min(2, links), links)
    def _(link):
        mix_link(link)

    load_data.wait()

    @pl.loop(1, team)
    def _(step):
        peer_rank = lax.rem(rank + step, team)

        @pl.loop(0, sectors)
        def _(of_sector):
            relay_copy(peer_rank, of_sector, peer_rank).wait_recv()

    @pl.loop(0, sectors)
    def _(index):
        frame = strips[pl.ds(index * team, team)].reshape(states, states)
        frames[index] = frame
        frames_t[index] = frame.astype(jnp.float32).T.astype(jnp.bfloat16)

    def turn(block, link):
        half_turn = jnp.dot(
            block, frames[couplings_ref[0, link]], preferred_element_type=jnp.float32
        )
        return jnp.dot(
            frames_t[couplings_ref[1, link]],
            half_turn.astype(jnp.bfloat16),
            preferred_element_type=jnp.float32,
        ).astype(jnp.bfloat16)

    def write(which, target, block):
        return pltpu.make_async_copy(
            done.at[which, block], target.at[block], out_sem.at[which, block]
        )

    @pl.loop(0, blocks)
    def _(block):
        done[0, block] = turn(data[block], lax.rem(block, links))
        write(0, normal_ref, block).start()

    @pl.loop(0, links)
    def _(link):
        kept_two(link).wait()

        @pl.loop(1, devices)
        def _(step):
            peer = lax.rem(me + step, devices)
            return_copy(link, peer, peer).wait_recv()

        @pl.loop(0, own)
        def _(place):
            block = place * links + link
            piece = landed[link, place].astype(jnp.float32).reshape(states, states)
            done[1, block] = turn(piece.astype(jnp.bfloat16), link)
            write(1, complementary_ref, block).start()

    @pl.loop(1, team)
    def _(step):
        peer_rank = lax.rem(rank + step, team)
        basis_copy(peer_rank, rank).wait_send()

        @pl.loop(0, sectors)
        def _(of_sector):
            relay_copy(peer_rank, of_sector, rank).wait_send()

    strip_copy(across, sector).wait_send()

    @pl.loop(1, half)
    def _(step):
        strip_copy(neighbour(step), sector).wait_send()
        strip_copy(neighbour(step), across).wait_send()

    @pl.loop(0, links)
    def _(link):
        @pl.loop(1, devices)
        def _(step):
            peer = lax.rem(me + step, devices)
            entry_copy(link, peer, me).wait_send()
            return_copy(link, peer, me).wait_send()

    @pl.loop(0, blocks)
    def _(block):
        write(0, normal_ref, block).wait()
        write(1, complementary_ref, block).wait()


def local(
    normal_ops,
    rotation_one,
    rotation_two,
    integrals,
    orbital_map,
    couplings,
    particles,
    state_counts,
):
    own_blocks, states, _ = normal_ops.shape
    orbits = integrals.shape[0]
    links = couplings.shape[0]
    sectors = state_counts.shape[0]
    devices = lax.axis_size("ops")
    own = own_blocks // links
    if own * links != own_blocks or states % (devices * SUB) or devices % sectors or sectors % 2:
        return local_general(
            normal_ops,
            rotation_one,
            rotation_two,
            integrals,
            orbital_map,
            couplings,
            particles,
            state_counts,
        )
    rows = states // devices
    team = devices // sectors
    wide = np.arange(orbits * SUB)
    widen = jnp.asarray(wide[:, None] // SUB == np.arange(orbits)[None, :], jnp.bfloat16)
    same = jnp.asarray(wide[:, None] % SUB == wide[None, :] % SUB, jnp.float32)
    anywhere = pl.BlockSpec(memory_space=pl.ANY)
    vmem = pl.BlockSpec(memory_space=pltpu.VMEM)
    smem = pl.BlockSpec(memory_space=pltpu.SMEM)
    dma = pltpu.SemaphoreType.DMA
    whole = (own_blocks, states, states)
    strip = rotation_one.shape
    return pl.pallas_call(
        functools.partial(sweep_kernel, devices),
        out_shape=(
            jax.ShapeDtypeStruct(whole, jnp.bfloat16),
            jax.ShapeDtypeStruct(whole, jnp.bfloat16),
        ),
        in_specs=[smem] * 4 + [vmem] * 3 + [anywhere] * 4,
        out_specs=(anywhere, anywhere),
        scratch_shapes=[
            pltpu.VMEM((links, devices, own, rows, states), jnp.bfloat16),
            pltpu.VMEM((devices, own, rows, states), jnp.bfloat16),
            pltpu.VMEM((links, own, devices, rows, states), jnp.bfloat16),
            pltpu.VMEM(whole, jnp.bfloat16),
            pltpu.VMEM(strip, jnp.bfloat16),
            pltpu.VMEM((team,) + strip, jnp.bfloat16),
            pltpu.VMEM(strip, jnp.bfloat16),
            pltpu.VMEM((devices,) + strip, jnp.bfloat16),
            pltpu.VMEM((sectors, states, states), jnp.bfloat16),
            pltpu.VMEM((sectors, states, states), jnp.bfloat16),
            pltpu.VMEM((2,) + whole, jnp.bfloat16),
            pltpu.VMEM((orbits, orbits), jnp.float32),
            dma((links, devices)),
            dma((links, devices)),
            dma((links, devices)),
            dma((links, devices)),
            dma((team,)),
            dma((team,)),
            dma((sectors, sectors)),
            dma((sectors,)),
            dma((team, sectors)),
            dma((team, sectors)),
            dma((links,)),
            dma((links,)),
            dma((4,)),
            dma,
            dma((2, own_blocks)),
        ],
        compiler_params=pltpu.CompilerParams(
            collective_id=0, has_side_effects=True, vmem_limit_bytes=LIMIT
        ),
    )(
        couplings.T,
        particles,
        state_counts,
        orbital_map,
        integrals,
        widen,
        same,
        normal_ops.reshape(own, links, devices, rows, states),
        normal_ops,
        rotation_one,
        rotation_two,
    )


def solution(mesh):
    placed = (
        P(("groups", "ops"), None, None),
        P(("groups", "ops"), None),
        P(("groups", "ops"), None),
        P("groups", None),
        P("groups"),
        P("groups", None),
        P("groups"),
        P("groups"),
    )
    return jax.shard_map(
        local,
        mesh=mesh,
        in_specs=placed,
        out_specs=(P(("groups", "ops"), None, None), P(("groups", "ops"), None, None)),
        check_vma=False,
    )
```

```python
import functools

import jax
import jax.numpy as jnp
import numpy as np
from jax import lax
from jax.experimental import pallas as pl
from jax.experimental.pallas import tpu as pltpu
from jax.sharding import PartitionSpec as P


def select_entries(lookup, wanted):
    matches = wanted[:, None] == jnp.arange(lookup.shape[0], dtype=jnp.int32)[None, :]
    return jnp.sum(jnp.where(matches, lookup[None, :], 0), axis=1)


def rotate(blocks, basis, live_mask, source, target):
    sectors = live_mask.shape[0]
    states = live_mask.shape[1]
    frames = basis.reshape(sectors, states, states)

    def single(packed):
        block_data, from_sector, to_sector = packed
        frame_in = lax.dynamic_index_in_dim(frames, from_sector, 0, keepdims=False)
        frame_out = lax.dynamic_index_in_dim(frames, to_sector, 0, keepdims=False)
        keep_in = lax.dynamic_index_in_dim(live_mask, from_sector, 0, keepdims=False)
        keep_out = lax.dynamic_index_in_dim(live_mask, to_sector, 0, keepdims=False)
        half_turn = (
            jnp.dot(block_data, frame_in, preferred_element_type=jnp.float32) * keep_in[None, :]
        ).astype(jnp.bfloat16)
        rotated = lax.dot_general(
            frame_out, half_turn, (((0,), (0,)), ((), ())), preferred_element_type=jnp.float32
        )
        return (rotated * keep_out[:, None]).astype(jnp.bfloat16)

    return lax.map(single, (blocks, source, target))


def fetch_second(rotation_two):
    return lax.all_gather(rotation_two, "ops", axis=0, tiled=True)


def local_general(
    normal_ops,
    rotation_one,
    rotation_two,
    integrals,
    orbital_map,
    couplings,
    particles,
    state_counts,
):
    own_blocks = normal_ops.shape[0]
    states = normal_ops.shape[1]
    orbits = integrals.shape[0]
    link_count = couplings.shape[0]
    devices = lax.axis_size("ops")
    live_mask = (jnp.arange(states, dtype=jnp.int32)[None, :] < state_counts[:, None]).astype(
        jnp.float32
    )
    block_ids = lax.axis_index("ops") * own_blocks + jnp.arange(own_blocks, dtype=jnp.int32)
    link_of = block_ids % link_count
    source = select_entries(couplings[:, 0], link_of)
    target = select_entries(couplings[:, 1], link_of)
    basis_two = None
    basis_one = lax.all_gather(rotation_one, "ops", axis=0, tiled=True)
    normal_mid = rotate(normal_ops, basis_one, live_mask, source, target)
    normal_next = None
    chosen = (orbital_map[:, None] == jnp.arange(orbits, dtype=jnp.int32)[None, :]).astype(
        jnp.float32
    )
    weights = jnp.dot(integrals, chosen.T, precision=lax.Precision.HIGHEST).astype(jnp.bfloat16)
    parity = (1 - 2 * (select_entries(particles, couplings[:, 0]) % 2)).astype(jnp.float32)
    piece_len = states * states // devices
    spread = normal_mid.reshape(own_blocks, devices, piece_len)
    received = lax.all_to_all(spread, "ops", split_axis=1, concat_axis=0, tiled=True)
    entries = received.shape[2]
    grouped = received.reshape(orbits, link_count, entries)
    mixture = jnp.einsum("ko,ocn->kcn", weights, grouped, preferred_element_type=jnp.float32)
    regrouped = lax.all_to_all(
        (mixture * parity[None, :, None])
        .astype(jnp.bfloat16)
        .reshape(orbits * link_count, 1, entries),
        "ops",
        split_axis=0,
        concat_axis=1,
        tiled=True,
    )
    complementary_mid = regrouped.reshape(own_blocks, states, states)
    basis_two = fetch_second(rotation_two)
    normal_next = rotate(normal_mid, basis_two, live_mask, source, target)
    complementary_next = rotate(complementary_mid, basis_two, live_mask, source, target)
    return (normal_next, complementary_next)


SUB = 8
LIMIT = 62 * 2**20


def greet(devices):
    me = lax.axis_index("ops")
    barrier = pltpu.get_barrier_semaphore()

    @pl.loop(1, devices)
    def _(step):
        peer = lax.rem(me + step, devices)
        pl.semaphore_signal(
            barrier, inc=1, device_id={"ops": peer}, device_id_type=pl.DeviceIdType.MESH
        )

    pl.semaphore_wait(barrier, devices - 1)
    return me


def send(source, place, send_sem, recv_sem, peer):
    return pltpu.make_async_remote_copy(
        src_ref=source,
        dst_ref=place,
        send_sem=send_sem,
        recv_sem=recv_sem,
        device_id={"ops": peer},
        device_id_type=pl.DeviceIdType.MESH,
    )


def sweep_kernel(
    devices,
    couplings_ref,
    particles_ref,
    counts_ref,
    orbital_ref,
    integrals_ref,
    widen_ref,
    same_ref,
    pieces_ref,
    ops_ref,
    one_ref,
    two_ref,
    normal_ref,
    complementary_ref,
    frames_out,
    frames_t_out,
    entries,
    stage,
    landed,
    data,
    one,
    two,
    own_frame,
    strips,
    frames,
    frames_t,
    done,
    chosen,
    send_one,
    recv_one,
    send_two,
    recv_two,
    send_basis,
    recv_basis,
    send_strip,
    recv_strip,
    send_relay,
    recv_relay,
    keep_one,
    keep_two,
    load_sem,
    stage_sem,
    out_sem,
):
    links, own, _, rows, states = landed.shape
    sectors = frames.shape[0]
    blocks = data.shape[0]
    team = devices // sectors
    me = greet(devices)
    sector, rank = lax.div(me, team), lax.rem(me, team)

    def basis_copy(peer_rank, slot):
        return send(
            two_ref,
            two.at[slot],
            send_basis.at[peer_rank],
            recv_basis.at[slot],
            sector * team + peer_rank,
        )

    half = sectors // 2
    across = lax.rem(sector + half, sectors)

    def strip_copy(peer_sector, slot):
        return send(
            strips.at[slot * team + rank],
            strips.at[slot * team + rank],
            send_strip.at[peer_sector, slot],
            recv_strip.at[slot],
            peer_sector * team + rank,
        )

    def neighbour(step):
        return lax.div(sector, half) * half + lax.rem(sector + step, half)

    def crossed(peer_sector):
        return lax.rem(peer_sector + half, sectors)

    def relay_copy(peer_rank, of_sector, of_rank):
        return send(
            strips.at[of_sector * team + of_rank],
            strips.at[of_sector * team + of_rank],
            send_relay.at[peer_rank, of_sector],
            recv_relay.at[of_rank, of_sector],
            sector * team + peer_rank,
        )

    def entry_copy(link, peer, slot):
        return send(
            pieces_ref.at[:, link, peer],
            entries.at[link, slot],
            send_one.at[link, peer],
            recv_one.at[link, slot],
            peer,
        )

    def return_copy(link, peer, slot):
        return send(
            entries.at[link, peer],
            landed.at[link, :, slot],
            send_two.at[link, peer],
            recv_two.at[link, slot],
            peer,
        )

    def kept_one(link):
        return pltpu.make_async_copy(
            pieces_ref.at[:, link, me], entries.at[link, me], keep_one.at[link]
        )

    def kept_two(link):
        return pltpu.make_async_copy(
            entries.at[link, me], landed.at[link, :, me], keep_two.at[link]
        )

    @pl.loop(1, team)
    def _(step):
        basis_copy(lax.rem(rank + step, team), rank).start()

    def send_entries(link):
        kept_one(link).start()

        @pl.loop(1, devices)
        def _(step):
            entry_copy(link, lax.rem(me + step, devices), me).start()

    send_entries(0)

    load_one = pltpu.make_async_copy(one_ref, one, load_sem.at[0])
    load_two = pltpu.make_async_copy(two_ref, two.at[rank], load_sem.at[1])
    load_data = pltpu.make_async_copy(ops_ref, data, load_sem.at[2])
    load_one.start()
    load_two.start()
    load_data.start()

    load_one.wait()
    load_two.wait()

    @pl.loop(1, team)
    def _(step):
        peer_rank = lax.rem(rank + step, team)
        basis_copy(peer_rank, peer_rank).wait_recv()

    columns = lax.broadcasted_iota(jnp.int32, (1, states), 1)
    live = (columns < counts_ref[sector]).astype(jnp.float32).astype(jnp.bfloat16)
    own_frame[...] = jnp.dot(
        one[...] * live,
        two[...].reshape(states, states) * live,
        preferred_element_type=jnp.float32,
    ).astype(jnp.bfloat16)
    own_strip = pltpu.make_async_copy(own_frame, strips.at[me], load_sem.at[3])
    own_strip.start()
    own_strip.wait()

    strip_copy(across, sector).start()

    @pl.loop(1, links)
    def _(link):
        send_entries(link)

    orbits = integrals_ref.shape[0]
    places = lax.broadcasted_iota(jnp.int32, (1, orbits), 1)
    for orbital in range(orbits):
        chosen[orbital : orbital + 1, :] = (places == orbital_ref[orbital]).astype(jnp.float32)
    weights = lax.dot_general(
        integrals_ref[...].astype(jnp.bfloat16),
        chosen[...].astype(jnp.bfloat16),
        (((1,), (1,)), ((), ())),
        preferred_element_type=jnp.float32,
    )
    weights = jnp.dot(
        widen_ref[...], weights.astype(jnp.bfloat16), preferred_element_type=jnp.float32
    )
    weights = lax.dot_general(
        weights.astype(jnp.bfloat16),
        widen_ref[...],
        (((1,), (1,)), ((), ())),
        preferred_element_type=jnp.float32,
    )
    weights = weights * same_ref[...]

    def mix_link(link):
        kept_one(link).wait()

        @pl.loop(1, devices)
        def _(step):
            peer = lax.rem(me + step, devices)
            entry_copy(link, peer, peer).wait_recv()

        parity = (1 - 2 * lax.rem(particles_ref[couplings_ref[0, link]], 2)).astype(jnp.float32)
        signed = (weights * parity).astype(jnp.bfloat16)
        for start in range(0, rows, SUB):
            piece = entries[link, :, :, start : start + SUB, :].astype(jnp.float32)
            piece = piece.reshape(devices * own * SUB, states).astype(jnp.bfloat16)
            total = jnp.dot(signed, piece, preferred_element_type=jnp.float32)
            stage[:, :, start : start + SUB, :] = total.reshape(devices, own, SUB, states).astype(
                jnp.bfloat16
            )
        moved = pltpu.make_async_copy(stage, entries.at[link], stage_sem)
        moved.start()
        moved.wait()
        kept_two(link).start()

        @pl.loop(1, devices)
        def _(step):
            return_copy(link, lax.rem(me + step, devices), me).start()

    mix_link(0)
    strip_copy(across, across).wait_recv()

    @pl.loop(1, half)
    def _(step):
        strip_copy(neighbour(step), sector).start()
        strip_copy(neighbour(step), across).start()

    @pl.loop(1, min(2, links))
    def _(link):
        mix_link(link)

    @pl.loop(1, half)
    def _(step):
        strip_copy(neighbour(step), neighbour(step)).wait_recv()
        strip_copy(neighbour(step), crossed(neighbour(step))).wait_recv()

    @pl.loop(1, team)
    def _(step):
        peer_rank = lax.rem(rank + step, team)

        @pl.loop(0, sectors)
        def _(of_sector):
            relay_copy(peer_rank, of_sector, rank).start()

    @pl.loop(min(2, links), links)
    def _(link):
        mix_link(link)

    load_data.wait()

    @pl.loop(1, team)
    def _(step):
        peer_rank = lax.rem(rank + step, team)

        @pl.loop(0, sectors)
        def _(of_sector):
            relay_copy(peer_rank, of_sector, peer_rank).wait_recv()

    @pl.loop(0, sectors)
    def _(index):
        frame = strips[pl.ds(index * team, team)].reshape(states, states)
        frames[index] = frame
        frames_t[index] = frame.astype(jnp.float32).T.astype(jnp.bfloat16)

    def turn(block, link):
        half_turn = jnp.dot(
            block, frames[couplings_ref[0, link]], preferred_element_type=jnp.float32
        )
        return jnp.dot(
            frames_t[couplings_ref[1, link]],
            half_turn.astype(jnp.bfloat16),
            preferred_element_type=jnp.float32,
        ).astype(jnp.bfloat16)

    def write(which, target, block):
        return pltpu.make_async_copy(
            done.at[which, block], target.at[block], out_sem.at[which, block]
        )

    @pl.loop(0, blocks)
    def _(block):
        done[0, block] = turn(data[block], lax.rem(block, links))
        write(0, normal_ref, block).start()

    frame_copies = (
        pltpu.make_async_copy(frames, frames_out, load_sem.at[4]),
        pltpu.make_async_copy(frames_t, frames_t_out, load_sem.at[5]),
    )
    for copy in frame_copies:
        copy.start()

    def collect(link, last):
        kept_two(link).wait()

        @pl.loop(1, devices)
        def _(step):
            peer = lax.rem(me + step, devices)
            return_copy(link, peer, peer).wait_recv()

        @pl.loop(0, own)
        def _(place):
            block = place * links + link
            piece = landed[link, place].astype(jnp.float32).reshape(states, states)
            piece = piece.astype(jnp.bfloat16)
            done[1, block] = piece if last else turn(piece, link)
            write(1, complementary_ref, block).start()

    @pl.loop(0, links - 1)
    def _(link):
        collect(link, False)

    collect(links - 1, True)
    for copy in frame_copies:
        copy.wait()

    @pl.loop(1, team)
    def _(step):
        peer_rank = lax.rem(rank + step, team)
        basis_copy(peer_rank, rank).wait_send()

        @pl.loop(0, sectors)
        def _(of_sector):
            relay_copy(peer_rank, of_sector, rank).wait_send()

    strip_copy(across, sector).wait_send()

    @pl.loop(1, half)
    def _(step):
        strip_copy(neighbour(step), sector).wait_send()
        strip_copy(neighbour(step), across).wait_send()

    @pl.loop(0, links)
    def _(link):
        @pl.loop(1, devices)
        def _(step):
            peer = lax.rem(me + step, devices)
            entry_copy(link, peer, me).wait_send()
            return_copy(link, peer, me).wait_send()

    @pl.loop(0, blocks)
    def _(block):
        write(0, normal_ref, block).wait()
        write(1, complementary_ref, block).wait()


def finish_kernel(
    links, ends_ref, normal_in, complementary_in, frame_in, frame_out, normal_ref, complementary_ref
):
    normal_ref[...] = normal_in[...]
    last = lax.rem(pl.program_id(0), links) == links - 1

    @pl.when(last)
    def _():
        half_turn = jnp.dot(complementary_in[0], frame_in[0], preferred_element_type=jnp.float32)
        complementary_ref[0] = jnp.dot(
            frame_out[0], half_turn.astype(jnp.bfloat16), preferred_element_type=jnp.float32
        ).astype(jnp.bfloat16)

    @pl.when(jnp.logical_not(last))
    def _():
        complementary_ref[...] = complementary_in[...]


def local(
    normal_ops,
    rotation_one,
    rotation_two,
    integrals,
    orbital_map,
    couplings,
    particles,
    state_counts,
):
    own_blocks, states, _ = normal_ops.shape
    orbits = integrals.shape[0]
    links = couplings.shape[0]
    sectors = state_counts.shape[0]
    devices = lax.axis_size("ops")
    own = own_blocks // links
    if own * links != own_blocks or states % (devices * SUB) or devices % sectors or sectors % 2:
        return local_general(
            normal_ops,
            rotation_one,
            rotation_two,
            integrals,
            orbital_map,
            couplings,
            particles,
            state_counts,
        )
    rows = states // devices
    team = devices // sectors
    wide = np.arange(orbits * SUB)
    widen = jnp.asarray(wide[:, None] // SUB == np.arange(orbits)[None, :], jnp.bfloat16)
    same = jnp.asarray(wide[:, None] % SUB == wide[None, :] % SUB, jnp.float32)
    anywhere = pl.BlockSpec(memory_space=pl.ANY)
    vmem = pl.BlockSpec(memory_space=pltpu.VMEM)
    smem = pl.BlockSpec(memory_space=pltpu.SMEM)
    dma = pltpu.SemaphoreType.DMA
    whole = (own_blocks, states, states)
    strip = rotation_one.shape
    swept = pl.pallas_call(
        functools.partial(sweep_kernel, devices),
        out_shape=(
            jax.ShapeDtypeStruct(whole, jnp.bfloat16),
            jax.ShapeDtypeStruct(whole, jnp.bfloat16),
            jax.ShapeDtypeStruct((sectors, states, states), jnp.bfloat16),
            jax.ShapeDtypeStruct((sectors, states, states), jnp.bfloat16),
        ),
        in_specs=[smem] * 4 + [vmem] * 3 + [anywhere] * 4,
        out_specs=(anywhere,) * 4,
        scratch_shapes=[
            pltpu.VMEM((links, devices, own, rows, states), jnp.bfloat16),
            pltpu.VMEM((devices, own, rows, states), jnp.bfloat16),
            pltpu.VMEM((links, own, devices, rows, states), jnp.bfloat16),
            pltpu.VMEM(whole, jnp.bfloat16),
            pltpu.VMEM(strip, jnp.bfloat16),
            pltpu.VMEM((team,) + strip, jnp.bfloat16),
            pltpu.VMEM(strip, jnp.bfloat16),
            pltpu.VMEM((devices,) + strip, jnp.bfloat16),
            pltpu.VMEM((sectors, states, states), jnp.bfloat16),
            pltpu.VMEM((sectors, states, states), jnp.bfloat16),
            pltpu.VMEM((2,) + whole, jnp.bfloat16),
            pltpu.VMEM((orbits, orbits), jnp.float32),
            dma((links, devices)),
            dma((links, devices)),
            dma((links, devices)),
            dma((links, devices)),
            dma((team,)),
            dma((team,)),
            dma((sectors, sectors)),
            dma((sectors,)),
            dma((team, sectors)),
            dma((team, sectors)),
            dma((links,)),
            dma((links,)),
            dma((6,)),
            dma,
            dma((2, own_blocks)),
        ],
        compiler_params=pltpu.CompilerParams(
            collective_id=0, has_side_effects=True, vmem_limit_bytes=LIMIT
        ),
    )(
        couplings.T,
        particles,
        state_counts,
        orbital_map,
        integrals,
        widen,
        same,
        normal_ops.reshape(own, links, devices, rows, states),
        normal_ops,
        rotation_one,
        rotation_two,
    )
    ends = couplings[links - 1]
    block_spec = pl.BlockSpec((1, states, states), lambda b, e: (b, 0, 0))
    return pl.pallas_call(
        functools.partial(finish_kernel, links),
        grid_spec=pltpu.PrefetchScalarGridSpec(
            num_scalar_prefetch=1,
            grid=(own_blocks,),
            in_specs=[
                block_spec,
                block_spec,
                pl.BlockSpec((1, states, states), lambda b, e: (e[0], 0, 0)),
                pl.BlockSpec((1, states, states), lambda b, e: (e[1], 0, 0)),
            ],
            out_specs=(block_spec, block_spec),
        ),
        out_shape=(
            jax.ShapeDtypeStruct(whole, jnp.bfloat16),
            jax.ShapeDtypeStruct(whole, jnp.bfloat16),
        ),
    )(ends, *swept)


def solution(mesh):
    placed = (
        P(("groups", "ops"), None, None),
        P(("groups", "ops"), None),
        P(("groups", "ops"), None),
        P("groups", None),
        P("groups"),
        P("groups", None),
        P("groups"),
        P("groups"),
    )
    return jax.shard_map(
        local,
        mesh=mesh,
        in_specs=placed,
        out_specs=(P(("groups", "ops"), None, None), P(("groups", "ops"), None, None)),
        check_vma=False,
    )
```
